512 devices in a mesh: mod: 2 (over z_hi), loop: 16 (over x, z_lo), line: 16 (over y, core).
Axes of the slice: x: 4, y: 8, z: 8 (z_hi: 2, z_lo: 4; z = z_hi * 4 + z_lo), core: 2. Of those that a mesh axis runs over, the one named last changes fastest.
Arguments:
- act: bfloat16 [2, 196608, 512], P('mod', ('loop', 'line'))
- dy: bfloat16 [2, 196608, 1280], P('mod', ('loop', 'line')), may hold values from -6 to 6
- w_out: bfloat16 [2, 512, 1280], P('mod'), may hold values from -0.15625 to 0.15625
- counts: int32 [2, 16, 16], P('mod', 'loop', 'line'), may hold values from 192 to 768, as said below
Outputs:
- grad_clipped: float32 [2, 512, 1280], P('mod', 'loop')
- hidden_grad: bfloat16 [2, 196608, 512], P('mod', ('loop', 'line'))
The draws below stay inside these ranges and needn't reach their ends.
Inputs may be any that keep to these rules, and one draw needn't show every extreme that they name: `counts`: in each tower some device has all 768 slots live.
All inputs are finite; a program needn't handle non-finite values.
Results may differ from the reference program's by a relative error of at most 0.001.
Values sent between devices are 32-bit elements; how exact they have to be, the bound alone decides.
A program may use at most 64 MiB of HBM per device.

```python
import jax
import jax.numpy as jnp
from jax import lax

H = 512
DB = 1280
ROWS = 768
TOTAL = 196608
N_MOD = 2
N_LOOP = 16
N_LINE = 16


def draw_act(key, part):
    total_rows = ROWS * N_LOOP * N_LINE
    first, second, third = jax.random.split(key, 3)
    place = (lax.broadcasted_iota(jnp.float32, (N_MOD, 1, H), 0) * H + lax.broadcasted_iota(jnp.float32, (N_MOD, 1, H), 2)) / (N_MOD * H)
    column_scale = jnp.exp(place * jnp.log(3.0)) * jnp.exp(jax.random.uniform(second, (N_MOD, 1, H), jnp.float32, 0.0, 1.15))
    row_scale = jnp.exp(jax.random.uniform(third, (N_MOD, total_rows, 1), jnp.float32, 0.0, 1.15))
    base = jax.random.normal(first, (N_MOD, total_rows, H), jnp.float32)
    return jnp.clip(base * row_scale * column_scale * 0.35, -8.0, 8.0).astype(jnp.bfloat16)


def draw_counts(key, part):
    first, second = jax.random.split(jax.random.fold_in(key, 11))
    values = jax.random.randint(first, (N_MOD, N_LOOP, N_LINE), ROWS // 4, ROWS + 1)
    chosen = jax.random.randint(second, (N_MOD, 1, 1), 0, N_LOOP * N_LINE)
    device = lax.broadcasted_iota(jnp.int32, (N_MOD, N_LOOP, N_LINE), 1) * N_LINE + lax.broadcasted_iota(jnp.int32, (N_MOD, N_LOOP, N_LINE), 2)
    return jnp.where(device == chosen, ROWS, values).astype(jnp.int32)


def shard_levels(stream_key, dims, shards, least, largest):
    gain, own = 1.0, jax.random.fold_in(stream_key, 6)
    for position, blocks in shards:
        heights = jnp.exp(jax.random.uniform(jax.random.fold_in(own, position), (blocks,), jnp.float32, least / len(shards), largest / len(shards)))
        gain = gain * jnp.repeat(heights, dims[position] // blocks).reshape([-1 if axis == position else 1 for axis in range(len(dims))])
    return gain


def scatter_about(key, dims, spread, most, cuts=(), kind=jnp.bfloat16):
    entries = jax.random.normal(key, dims, jnp.float32) * spread
    if len(cuts) > 0:
        entries = shard_levels(key, dims, cuts, -0.22, 0.18) * entries
    return jnp.clip(entries, min=-most, max=most).astype(kind)


def setup_inputs(seed: int = 0) -> dict:
    key_list = jax.random.split(jax.random.key(seed), 5)
    act = draw_act(jax.random.fold_in(key_list[4], 71), 0)
    dy = scatter_about(key_list[1], (N_MOD, TOTAL, DB), 1.0, 6.0, ((0, 2), (1, 256)))
    w_out = scatter_about(key_list[2], (N_MOD, H, DB), DB ** -0.5, 0.15625, ((0, 2),))
    counts = draw_counts(jax.random.fold_in(key_list[4], 71), 0)
    return {"act": act, "dy": dy, "w_out": w_out, "counts": counts}


def reference(act, dy, w_out, counts):
    flat = counts.reshape(N_MOD, N_LOOP * N_LINE)
    limit = jnp.repeat(flat, ROWS, axis=1)
    within = (jnp.arange(ROWS * N_LOOP * N_LINE, dtype=jnp.int32) % ROWS)[None, :]
    live = (within < limit)[:, :, None]
    masked = jnp.where(live, act, jnp.zeros_like(act))
    grads = []
    hiddens = []
    for tower in range(N_MOD):
        grads.append(lax.dot_general(masked[tower], dy[tower], (((0,), (0,)), ((), ())), preferred_element_type=jnp.float32))
        back = lax.dot_general(dy[tower], w_out[tower], (((1,), (1,)), ((), ())), preferred_element_type=jnp.float32)
        hiddens.append(jnp.where(live[tower], back, jnp.zeros_like(back)).astype(jnp.bfloat16))
    grad = jnp.stack(grads)
    total = jnp.sum(grad * grad)
    factor = 1.0 / jnp.sqrt(total / (N_MOD * H * DB) + 1e-06)
    return (grad * factor, jnp.stack(hiddens))
```

```python
import functools

import jax
import jax.numpy as jnp
from jax import lax
from jax.experimental import pallas as pl
from jax.experimental.pallas import tpu as pltpu
from jax.sharding import PartitionSpec as P

MESH = pl.DeviceIdType.MESH
F32 = jnp.float32
BF16 = jnp.bfloat16

NX, NZ, NY, NM = 4, 4, 8, 2
NLINE = NY * 2
COLS = 256
UNITS = 5
SLOTS = 3


def remote(src, dst, ssem, rsem, peer):
    return pltpu.make_async_remote_copy(
        src_ref=src, dst_ref=dst, send_sem=ssem, recv_sem=rsem, device_id=peer, device_id_type=MESH
    )


def kernel(
    entries,
    cnt_ref, act_hbm, dy_hbm, w_hbm,
    out_ref, hid_hbm,
    act_v, dy_v, w_v, hid_v, act_t,
    pair_s, pair_r, own, xr, xf, zr, yr, ag, s1, s2,
    ld_sem, hid_sem,
    pair_ss, pair_rs, x_ss, x_rs, z_ss, z_rs, y_ss, y_rs,
    ag_ss, ag_rs, s1_ss, s1_rs, s2_ss, s2_rs,
):
    mod = lax.axis_index("mod")
    loop = lax.axis_index("loop")
    line = lax.axis_index("line")
    x, z = loop // NZ, lax.rem(loop, NZ)
    y, core = line // 2, lax.rem(line, 2)
    rows = act_v.shape[0]
    hidden = act_v.shape[1]

    def at(dm=0, dx=0, dz=0, dline=0):
        m2 = lax.rem(mod + dm, NM) if dm else mod
        x2 = lax.rem(x + dx, NX) if dx else x
        z2 = lax.rem(z + dz, NZ) if dz else z
        l2 = lax.rem(line + dline, NLINE) if dline else line
        return (m2, x2 * NZ + z2, l2)

    partner = (mod, loop, y * 2 + (1 - core))

    barrier = pltpu.get_barrier_semaphore()
    offsets = [(dm, dx, dz) for dm in range(NM) for dx in range(NX) for dz in range(NZ)][1:]
    for dl in range(1, NLINE):
        pl.semaphore_signal(barrier, inc=1, device_id=at(dline=dl), device_id_type=MESH)
    for dm, dx, dz in offsets:
        pl.semaphore_signal(barrier, inc=1, device_id=at(dm, dx, dz), device_id_type=MESH)

    first = 3 * (1 - core)
    mine = 3 * core
    order = [first, mine, first + 1, mine + 1, 2]
    load_act = pltpu.make_async_copy(act_hbm.at[0], act_v, ld_sem.at[0])
    load_act.start()
    load_dy = []
    for j, u in enumerate(order):
        src = dy_hbm.at[0, :, pl.ds(pl.multiple_of(u * COLS, COLS), COLS)]
        copy = pltpu.make_async_copy(src, dy_v.at[u], ld_sem.at[1 + j])
        copy.start()
        load_dy.append(copy)
    load_w = []
    for u in range(UNITS):
        src = w_hbm.at[0, :, pl.ds(u * COLS, COLS)]
        copy = pltpu.make_async_copy(src, w_v.at[u], ld_sem.at[6 + u])
        copy.start()
        load_w.append(copy)

    count = cnt_ref[0, 0, 0]
    load_act.wait()
    flipped = act_v[...].T
    alive = lax.broadcasted_iota(jnp.int32, (hidden, rows), 1) < count
    act_t[...] = jnp.where(alive, flipped, jnp.zeros_like(flipped))

    def product(u, dst):
        half = hidden // 2
        for i in range(2):
            acc = jnp.dot(act_t[i * half:(i + 1) * half, :], dy_v[u], preferred_element_type=F32)
            tiles = acc.reshape(NX // 2, NZ, 4, 8, COLS)
            dst[2 * i:2 * i + 2, :, 0:4] = tiles[..., 0:128]
            dst[2 * i:2 * i + 2, :, 4:8] = tiles[..., 128:256]

    sends = [[], [], [], []]

    def pair_copy(k):
        return remote(pair_s.at[k], pair_r.at[k], pair_ss.at[k], pair_rs.at[k], partner)

    def x_copy(k, i):
        right, left = lax.rem(x + 1, NX), lax.rem(x + 3, NX)
        across = lax.rem(x + 2, NX)
        lo, hi = pl.ds(0, 4), pl.ds(4, 4)
        src, dst, dx = (
            (own.at[k, across, :, lo], xr.at[k, 0], 1),
            (own.at[k, across, :, hi], xr.at[k, 1], 3),
            (own.at[k, right, :, hi], xf.at[k, 1], 1),
            (own.at[k, left, :, lo], xf.at[k, 2], 3),
            (own.at[k, right, :, lo], xf.at[k, 0], 1),
            (own.at[k, left, :, hi], xf.at[k, 3], 3),
        )[i]
        return remote(src, dst, x_ss.at[k, i], x_rs.at[k, i], at(dx=dx))

    def z_copy(k, d):
        src = own.at[k, x, lax.rem(z + d, NZ)]
        return remote(src, zr.at[k, d - 1], z_ss.at[k, d - 1], z_rs.at[k, d - 1], at(dz=d))

    def y_copy(k, d):
        src = own.at[k, x, z, lax.rem(y + d, NY)]
        return remote(src, yr.at[k, d - 1], y_ss.at[k, d - 1], y_rs.at[k, d - 1], at(dline=2 * d))

    def s1_copy(i):
        return remote(s1.at[0], s1.at[i + 1], s1_ss.at[i], s1_rs.at[i], at(*offsets[i]))

    def s2_copy(d):
        return remote(s2.at[0], s2.at[d], s2_ss.at[d - 1], s2_rs.at[d - 1], at(dline=d))

    def ag_copy(d):
        shard = ag.at[core, y]
        return remote(shard, shard, ag_ss.at[d - 1], ag_rs.at[d - 1], at(dline=d))

    def start(k, make, *args):
        make(*args).start()
        sends[k].append((make, args))

    def e2(k):
        pair_copy(k).wait_recv()
        right, left = lax.rem(x + 1, NX), lax.rem(x + 3, NX)
        across = lax.rem(x + 2, NX)
        own[k, across] = own[k, across] + pair_r[k, across]
        start(k, x_copy, k, 0)
        start(k, x_copy, k, 1)
        own[k, right] = own[k, right] + pair_r[k, right]
        start(k, x_copy, k, 2)
        own[k, left] = own[k, left] + pair_r[k, left]
        start(k, x_copy, k, 3)
        own[k, x] = own[k, x] + pair_r[k, x]

    def e3(k):
        right, left = lax.rem(x + 1, NX), lax.rem(x + 3, NX)
        x_copy(k, 0).wait_recv()
        own[k, right, :, 0:4] = own[k, right, :, 0:4] + xr[k, 0]
        start(k, x_copy, k, 4)
        x_copy(k, 1).wait_recv()
        own[k, left, :, 4:8] = own[k, left, :, 4:8] + xr[k, 1]
        start(k, x_copy, k, 5)

    def e4(k):
        x_copy(k, 3).wait_recv()
        x_copy(k, 4).wait_recv()
        own[k, x, :, 0:4] = own[k, x, :, 0:4] + xf[k, 0] + xf[k, 2]
        x_copy(k, 2).wait_recv()
        x_copy(k, 5).wait_recv()
        own[k, x, :, 4:8] = own[k, x, :, 4:8] + xf[k, 1] + xf[k, 3]
        for d in range(1, NZ):
            start(k, z_copy, k, d)

    def e5(k):
        for d in range(1, NZ):
            z_copy(k, d).wait_recv()
        own[k, x, z] = own[k, x, z] + zr[k, 0] + zr[k, 1] + zr[k, 2]
        for d in range(1, NY):
            start(k, y_copy, k, d)

    def e6(k):
        for d in range(1, NY):
            y_copy(k, d).wait_recv()
        total = own[k, x, z, y]
        for d in range(1, NY):
            total = total + yr[k, d - 1]
        ag[core, y, k] = total

    def step(event, k):
        if k < 2:
            event(k)
        else:
            pl.when(core == 0)(lambda: event(k))

    def hidden_rows(i):
        if i == 0:
            for copy in load_w:
                copy.wait()
        n = rows // 3
        part = pl.ds(i * n, n)
        back = jnp.zeros((n, hidden), F32)
        for u in range(UNITS):
            back = back + lax.dot_general(
                dy_v[u, i * n:(i + 1) * n, :], w_v[u], (((1,), (1,)), ((), ())),
                preferred_element_type=F32,
            )
        alive = lax.broadcasted_iota(jnp.int32, (n, hidden), 0) + i * n < count
        hid_v[i * n:(i + 1) * n, :] = jnp.where(alive, back, jnp.zeros_like(back)).astype(BF16)
        copy = pltpu.make_async_copy(hid_v.at[part], hid_hbm.at[0, part], hid_sem.at[i])
        copy.start()
        return copy

    load_dy[0].wait()
    product(order[0], pair_s.at[0])
    pl.semaphore_wait(barrier, NLINE - 1 + len(offsets))
    start(3, pair_copy, 0)
    load_dy[1].wait()
    product(order[1], own.at[0])
    load_dy[2].wait()
    product(order[2], pair_s.at[1])
    start(3, pair_copy, 1)
    e2(0)
    load_dy[3].wait()
    product(order[3], own.at[1])
    load_dy[4].wait()

    @pl.when(core == 0)
    def _():
        product(2, own.at[2])

    @pl.when(core == 1)
    def _():
        product(2, pair_s.at[2])
        pair_copy(2).start()
        ag[core, y, 2] = jnp.zeros((8, 128), F32)

    e3(0)
    e2(1)
    saved = [hidden_rows(0)]
    e4(0)
    e3(1)
    step(e2, 2)
    saved.append(hidden_rows(1))
    e5(0)
    e4(1)
    step(e3, 2)
    saved.append(hidden_rows(2))
    step(e4, 2)
    e5(1)
    e6(0)
    step(e5, 2)
    e6(1)
    step(e6, 2)

    shard = ag[core, y]
    s1[0] = jnp.sum(jnp.sum(shard * shard, axis=0), axis=0, keepdims=True)
    for i in range(len(offsets)):
        start(3, s1_copy, i)

    for dl in range(1, NLINE):
        start(3, ag_copy, dl)
    for i in range(len(offsets)):
        s1_copy(i).wait_recv()
    s2[0] = jnp.sum(s1[...], axis=0)
    for dl in range(1, NLINE):
        start(3, s2_copy, dl)
    for dl in range(1, NLINE):
        ag_copy(dl).wait_recv()
    for dl in range(1, NLINE):
        s2_copy(dl).wait_recv()
    total = jnp.sum(jnp.sum(s2[...], axis=0), axis=-1, keepdims=True)
    factor = 1.0 / jnp.sqrt(total / entries + 1e-06)
    for u in range(UNITS):
        for q in range(NY):
            r, c = (q % 4) * 8, u * COLS + (q // 4) * 128
            out_ref[0, r:r + 8, c:c + 128] = ag[u // 3, q, u % 3] * factor

    for make, args in sends[0] + sends[1] + sends[3]:
        make(*args).wait_send()

    @pl.when(core == 0)
    def _():
        for make, args in sends[2]:
            make(*args).wait_send()

    @pl.when(core == 1)
    def _():
        pair_copy(2).wait_send()

    for copy in saved:
        copy.wait()


def on_device(act, dy, w_out, counts):
    rows, hidden = act.shape[1:]
    block = w_out.shape[2]
    entries = NM * hidden * block
    dma = pltpu.SemaphoreType.DMA
    tile = (8, 128)
    unit = (NX, NZ, NY) + tile
    scratch = [
        pltpu.VMEM((rows, hidden), BF16),
        pltpu.VMEM((UNITS, rows, COLS), BF16),
        pltpu.VMEM((UNITS, hidden, COLS), BF16),
        pltpu.VMEM((rows, hidden), BF16),
        pltpu.VMEM((hidden, rows), BF16),
        pltpu.VMEM((SLOTS,) + unit, F32),
        pltpu.VMEM((SLOTS,) + unit, F32),
        pltpu.VMEM((SLOTS,) + unit, F32),
        pltpu.VMEM((SLOTS, 2, NZ, 4) + tile, F32),
        pltpu.VMEM((SLOTS, 4, NZ, 4) + tile, F32),
        pltpu.VMEM((SLOTS, NZ - 1, NY) + tile, F32),
        pltpu.VMEM((SLOTS, NY - 1) + tile, F32),
        pltpu.VMEM((2, NY, SLOTS) + tile, F32),
        pltpu.VMEM((NM * NX * NZ, 1, 128), F32),
        pltpu.VMEM((NLINE, 1, 128), F32),
        dma((11,)), dma((3,)),
        dma((SLOTS,)), dma((SLOTS,)),
        dma((SLOTS, 6)), dma((SLOTS, 6)),
        dma((SLOTS, NZ - 1)), dma((SLOTS, NZ - 1)),
        dma((SLOTS, NY - 1)), dma((SLOTS, NY - 1)),
        dma((NLINE - 1,)), dma((NLINE - 1,)),
        dma((NM * NX * NZ - 1,)), dma((NM * NX * NZ - 1,)),
        dma((NLINE - 1,)), dma((NLINE - 1,)),
    ]
    clipped, back = pl.pallas_call(
        functools.partial(kernel, float(entries)),
        out_shape=(
            jax.ShapeDtypeStruct((1, hidden // (NX * NZ), block), F32),
            jax.ShapeDtypeStruct((1, rows, hidden), BF16),
        ),
        in_specs=[
            pl.BlockSpec(memory_space=pltpu.SMEM),
            pl.BlockSpec(memory_space=pl.ANY),
            pl.BlockSpec(memory_space=pl.ANY),
            pl.BlockSpec(memory_space=pl.ANY),
        ],
        out_specs=(pl.BlockSpec(memory_space=pltpu.VMEM), pl.BlockSpec(memory_space=pl.ANY)),
        scratch_shapes=scratch,
        compiler_params=pltpu.CompilerParams(
            collective_id=0, has_side_effects=True, vmem_limit_bytes=48 * 1024 * 1024
        ),
        name="grad_reduce",
    )(counts, act, dy, w_out)
    return clipped, back


def solution(mesh):
    in_specs = (
        P("mod", ("loop", "line"), None),
        P("mod", ("loop", "line"), None),
        P("mod", None, None),
        P("mod", "loop", "line"),
    )
    out_specs = (P("mod", "loop", None), P("mod", ("loop", "line"), None))
    return jax.shard_map(
        on_device, mesh=mesh, in_specs=in_specs, out_specs=out_specs, check_vma=False
    )
```

```python
import functools

import jax
import jax.numpy as jnp
from jax import lax
from jax.experimental import pallas as pl
from jax.experimental.pallas import tpu as pltpu
from jax.sharding import PartitionSpec as P

MESH = pl.DeviceIdType.MESH
F32 = jnp.float32
BF16 = jnp.bfloat16

NX, NZ, NY, NM = 4, 4, 8, 2
NLINE = NY * 2
COLS = 256
UNITS = ((0, 1, 2), (3, 4))
TILE = (8, 128)


def remote(src, dst, ssem, rsem, peer):
    return pltpu.make_async_remote_copy(
        src_ref=src, dst_ref=dst, send_sem=ssem, recv_sem=rsem, device_id=peer, device_id_type=MESH
    )


def kernel(
    entries,
    cnt, act_hbm, dy_hbm, w_hbm,
    out_ref, hid_ref,
    act_v, dy_v, w_v, act_t,
    pair_s, pair_r, own, xr, xf, zr, yr,
    zr1, xr2, yr1, xr3, zr3,
    ag, s1, s2,
    ld_sem, gossip,
    pair_ss, pair_rs, x_ss, x_rs, z_ss, z_rs, y_ss, y_rs,
    zr1_ss, zr1_rs, xr2_ss, xr2_rs, yr1_ss, yr1_rs, xr3_ss, xr3_rs, zr3_ss, zr3_rs,
    ag_ss, ag_rs, s1_ss, s1_rs, s2_ss, s2_rs,
):
    mod = lax.axis_index("mod")
    loop = lax.axis_index("loop")
    line = lax.axis_index("line")
    x, z = loop // NZ, lax.rem(loop, NZ)
    y, core = line // 2, lax.rem(line, 2)
    rows, hidden = act_v.shape

    def at(dm=0, dx=0, dz=0, dline=0):
        m2 = lax.rem(mod + dm, NM) if dm else mod
        x2 = lax.rem(x + dx, NX) if dx else x
        z2 = lax.rem(z + dz, NZ) if dz else z
        l2 = lax.rem(line + dline, NLINE) if dline else line
        return (m2, x2 * NZ + z2, l2)

    def along_z(d):
        ring = lax.rem(mod * NZ + z + d, NM * NZ)
        return (ring // NZ, x * NZ + lax.rem(ring, NZ), line)

    partner = (mod, loop, y * 2 + (1 - core))
    near_x = [at(dx=1), at(dx=NX - 1)]
    near_yz = [at(dline=2), at(dline=NLINE - 2), along_z(1), along_z(NM * NZ - 1)]

    barrier = pltpu.get_barrier_semaphore()
    for peer in [partner] + near_x + near_yz:
        pl.semaphore_signal(barrier, inc=1, device_id=peer, device_id_type=MESH)

    def tell(r):
        for peer in (near_x + near_yz if r == 0 else near_yz):
            pl.semaphore_signal(gossip.at[r], inc=1, device_id=peer, device_id_type=MESH)

    def hear(r):
        pl.semaphore_wait(gossip.at[r], 6 if r == 0 else 4)

    right, left = lax.rem(x + 1, NX), lax.rem(x + 3, NX)
    across = lax.rem(x + 2, NX)
    lo, hi = pl.ds(0, 4), pl.ds(4, 4)

    def pair_copy(k):
        return remote(pair_s.at[k], pair_r.at[k], pair_ss.at[k], pair_rs.at[k], partner)

    def x_copy(k, i):
        src, dst, dx = (
            (own.at[k, across, :, lo], xr.at[k, 0], 1),
            (own.at[k, across, :, hi], xr.at[k, 1], 3),
            (own.at[k, right, :, hi], xf.at[k, 1], 1),
            (own.at[k, left, :, lo], xf.at[k, 2], 3),
            (own.at[k, right, :, lo], xf.at[k, 0], 1),
            (own.at[k, left, :, hi], xf.at[k, 3], 3),
        )[i]
        return remote(src, dst, x_ss.at[k, i], x_rs.at[k, i], at(dx=dx))

    def z_copy(k, d):
        src = own.at[k, x, lax.rem(z + d, NZ)]
        return remote(src, zr.at[k, d - 1], z_ss.at[k, d - 1], z_rs.at[k, d - 1], at(dz=d))

    def y_copy(k, d):
        src = own.at[k, x, z, lax.rem(y + d, NY)]
        return remote(src, yr.at[k, d - 1], y_ss.at[k, d - 1], y_rs.at[k, d - 1], at(dline=2 * d))

    def zr1_copy(k, d):
        src = own.at[k, :, lax.rem(z + d, NZ)]
        return remote(src, zr1.at[d - 1], zr1_ss.at[d - 1], zr1_rs.at[d - 1], at(dz=d))

    def xr2_copy(k, d):
        src = own.at[k, lax.rem(x + d, NX), z]
        return remote(src, xr2.at[d - 1], xr2_ss.at[d - 1], xr2_rs.at[d - 1], at(dx=d))

    def yr1_copy(k, d):
        src = own.at[k, :, :, lax.rem(y + d, NY)]
        return remote(src, yr1.at[d - 1], yr1_ss.at[d - 1], yr1_rs.at[d - 1], at(dline=2 * d))

    def xr3_copy(k, d):
        src = own.at[k, lax.rem(x + d, NX), :, y]
        return remote(src, xr3.at[d - 1], xr3_ss.at[d - 1], xr3_rs.at[d - 1], at(dx=d))

    def zr3_copy(k, d):
        src = own.at[k, x, lax.rem(z + d, NZ), y]
        return remote(src, zr3.at[d - 1], zr3_ss.at[d - 1], zr3_rs.at[d - 1], at(dz=d))

    def run(c):
        mine, theirs = UNITS[c], UNITS[1 - c]
        sent = []

        def start(make, *args):
            make(*args).start()
            sent.append((make, args))

        def arrive(make, k, n):
            for d in range(1, n):
                make(k, d).wait_recv()

        order = (3, 0, 4, 2, 1) if c == 0 else (0, 3, 2, 4, 1)
        load_act = pltpu.make_async_copy(act_hbm.at[0], act_v, ld_sem.at[0])
        load_act.start()
        load_dy, load_w = {}, []
        for u in order:
            src = dy_hbm.at[0, :, pl.ds(u * COLS, COLS)]
            load_dy[u] = pltpu.make_async_copy(src, dy_v.at[u], ld_sem.at[1 + u])
            load_dy[u].start()
        for u in order:
            src = w_hbm.at[0, :, pl.ds(u * COLS, COLS)]
            load_w.append(pltpu.make_async_copy(src, w_v.at[u], ld_sem.at[6 + u]))
            load_w[-1].start()

        count = cnt[0, 0, 0]
        load_act.wait()
        flipped = act_v[...].T
        alive = lax.broadcasted_iota(jnp.int32, (hidden, rows), 1) < count
        act_t[...] = jnp.where(alive, flipped, jnp.zeros_like(flipped))

        def product(u):
            load_dy[u].wait()
            dst = own.at[mine.index(u)] if u in mine else pair_s.at[theirs.index(u)]
            half = hidden // 2
            for i in range(2):
                acc = jnp.dot(
                    act_t[i * half:(i + 1) * half, :], dy_v[u], preferred_element_type=F32
                )
                tiles = acc.reshape(NX // 2, NZ, 4, 8, COLS)
                dst[2 * i:2 * i + 2, :, 0:4] = tiles[..., 0:128]
                dst[2 * i:2 * i + 2, :, 4:8] = tiles[..., 128:256]

        def hidden_rows(i):
            if i == 0:
                for copy in load_w:
                    copy.wait()
            n = rows // 3
            back = jnp.zeros((n, hidden), F32)
            for u in range(5):
                back = back + lax.dot_general(
                    dy_v[u, i * n:(i + 1) * n, :], w_v[u], (((1,), (1,)), ((), ())),
                    preferred_element_type=F32,
                )
            keep = lax.broadcasted_iota(jnp.int32, (n, hidden), 0) + i * n < count
            hid_ref[0, i * n:(i + 1) * n, :] = jnp.where(keep, back, jnp.zeros_like(back)).astype(BF16)

        def e2(k):
            pair_copy(k).wait_recv()
            own[k, across] = own[k, across] + pair_r[k, across]
            start(x_copy, k, 0)
            start(x_copy, k, 1)
            own[k, right] = own[k, right] + pair_r[k, right]
            start(x_copy, k, 2)
            own[k, left] = own[k, left] + pair_r[k, left]
            start(x_copy, k, 3)
            own[k, x] = own[k, x] + pair_r[k, x]

        def e3(k):
            x_copy(k, 0).wait_recv()
            own[k, right, :, 0:4] = own[k, right, :, 0:4] + xr[k, 0]
            start(x_copy, k, 4)
            x_copy(k, 1).wait_recv()
            own[k, left, :, 4:8] = own[k, left, :, 4:8] + xr[k, 1]
            start(x_copy, k, 5)

        def e4(k):
            x_copy(k, 3).wait_recv()
            x_copy(k, 4).wait_recv()
            own[k, x, :, 0:4] = own[k, x, :, 0:4] + xf[k, 0] + xf[k, 2]
            x_copy(k, 2).wait_recv()
            x_copy(k, 5).wait_recv()
            own[k, x, :, 4:8] = own[k, x, :, 4:8] + xf[k, 1] + xf[k, 3]
            for d in (2, 1, 3):
                start(z_copy, k, d)

        def e5(k):
            arrive(z_copy, k, NZ)
            own[k, x, z] = own[k, x, z] + zr[k, 0] + zr[k, 1] + zr[k, 2]
            for d in (4, 3, 5, 2, 6, 1, 7):
                start(y_copy, k, d)

        def e6(k):
            arrive(y_copy, k, NY)
            total = own[k, x, z, y]
            for d in range(1, NY):
                total = total + yr[k, d - 1]
            ag[c, y, k] = total

        def a1(k):
            pair_copy(k).wait_recv()
            for d in (2, 1, 3, 0):
                to = lax.rem(z + d, NZ)
                own[k, :, to] = own[k, :, to] + pair_r[k, :, to]
                if d:
                    start(zr1_copy, k, d)

        def a2(k):
            arrive(zr1_copy, k, NZ)
            own[k, :, z] = own[k, :, z] + zr1[0] + zr1[1] + zr1[2]
            for d in (2, 1, 3):
                start(xr2_copy, k, d)

        def a3(k):
            arrive(xr2_copy, k, NX)
            own[k, x, z] = own[k, x, z] + xr2[0] + xr2[1] + xr2[2]
            for d in (4, 3, 5, 2, 6, 1, 7):
                start(y_copy, k, d)

        def b1(k):
            pair_copy(k).wait_recv()
            for d in (4, 3, 5, 2, 6, 1, 7, 0):
                to = lax.rem(y + d, NY)
                own[k, :, :, to] = own[k, :, :, to] + pair_r[k, :, :, to]
                if d:
                    start(yr1_copy, k, d)

        def b2(k):
            arrive(yr1_copy, k, NY)
            total = own[k, :, :, y]
            for d in range(1, NY):
                total = total + yr1[d - 1]
            own[k, :, :, y] = total
            for d in (2, 1, 3):
                start(xr3_copy, k, d)

        def b3(k):
            arrive(xr3_copy, k, NX)
            own[k, x, :, y] = own[k, x, :, y] + xr3[0] + xr3[1] + xr3[2]
            for d in (2, 1, 3):
                start(zr3_copy, k, d)

        def b4(k):
            arrive(zr3_copy, k, NZ)
            ag[c, y, k] = own[k, x, z, y] + zr3[0] + zr3[1] + zr3[2]

        product(order[0])
        pl.semaphore_wait(barrier, 7)
        start(pair_copy, 0)
        tell(0)
        product(order[1])
        hear(0)
        tell(1)
        e2(0)
        product(order[2])
        start(pair_copy, 1 if c == 0 else 2)
        hear(1)
        tell(2)
        product(order[3])
        hear(2)
        if c == 0:
            b1(2)
            product(order[4])
            e3(0)
            e2(1)
            hidden_rows(0)
            hidden_rows(1)
            e4(0)
            e3(1)
            hidden_rows(2)
            e4(1)
            e5(0)
            e5(1)
            b2(2)
            e6(0)
            b3(2)
            e6(1)
            b4(2)
        else:
            ag[1, y, 2] = jnp.zeros(TILE, F32)
            a1(1)
            product(order[4])
            start(pair_copy, 1)
            e3(0)
            hidden_rows(0)
            hidden_rows(1)
            e4(0)
            hidden_rows(2)
            e5(0)
            a2(1)
            a3(1)
            e6(0)
            e6(1)
        for make, args in sent:
            make(*args).wait_send()

    pl.when(core == 0)(functools.partial(run, 0))
    pl.when(core == 1)(functools.partial(run, 1))

    offsets = [(dm, dx, dz) for dm in range(NM) for dx in range(NX) for dz in range(NZ)][1:]

    def s1_copy(i):
        return remote(s1.at[0], s1.at[i + 1], s1_ss.at[i], s1_rs.at[i], at(*offsets[i]))

    def s2_copy(d):
        return remote(s2.at[0], s2.at[d], s2_ss.at[d - 1], s2_rs.at[d - 1], at(dline=d))

    def ag_copy(d):
        shard = ag.at[core, y]
        return remote(shard, shard, ag_ss.at[d - 1], ag_rs.at[d - 1], at(dline=d))

    shard = ag[core, y]
    s1[0] = jnp.sum(jnp.sum(shard * shard, axis=0), axis=0, keepdims=True)
    for i in range(len(offsets)):
        s1_copy(i).start()
    for d in range(1, NLINE):
        ag_copy(d).start()
    for i in range(len(offsets)):
        s1_copy(i).wait_recv()
    s2[0] = jnp.sum(s1[...], axis=0)
    for d in range(1, NLINE):
        s2_copy(d).start()
    for d in range(1, NLINE):
        ag_copy(d).wait_recv()
    for i in range(len(offsets)):
        s1_copy(i).wait_send()
    for d in range(1, NLINE):
        ag_copy(d).wait_send()
    for d in range(1, NLINE):
        s2_copy(d).wait_recv()
    total = jnp.sum(jnp.sum(s2[...], axis=0), axis=-1, keepdims=True)
    factor = 1.0 / jnp.sqrt(total / entries + 1e-06)
    for c in range(2):
        for k, u in enumerate(UNITS[c]):
            for q in range(NY):
                r, col = (q % 4) * 8, u * COLS + (q // 4) * 128
                out_ref[0, r:r + 8, col:col + 128] = ag[c, q, k] * factor
    for d in range(1, NLINE):
        s2_copy(d).wait_send()


def store(a_ref, b_ref, a_out, b_out, sem):
    first = pltpu.make_async_copy(b_ref, b_out, sem.at[0])
    second = pltpu.make_async_copy(a_ref, a_out, sem.at[1])
    first.start()
    second.start()
    first.wait()
    second.wait()


def on_device(act, dy, w_out, counts):
    rows, hidden = act.shape[1:]
    block = w_out.shape[2]
    entries = NM * hidden * block
    dma = pltpu.SemaphoreType.DMA
    slots = 3
    unit = (NX, NZ, NY) + TILE
    scratch = [
        pltpu.VMEM((rows, hidden), BF16),
        pltpu.VMEM((5, rows, COLS), BF16),
        pltpu.VMEM((5, hidden, COLS), BF16),
        pltpu.VMEM((hidden, rows), BF16),
        pltpu.VMEM((slots,) + unit, F32),
        pltpu.VMEM((slots,) + unit, F32),
        pltpu.VMEM((slots,) + unit, F32),
        pltpu.VMEM((2, 2, NZ, 4) + TILE, F32),
        pltpu.VMEM((2, 4, NZ, 4) + TILE, F32),
        pltpu.VMEM((2, NZ - 1, NY) + TILE, F32),
        pltpu.VMEM((2, NY - 1) + TILE, F32),
        pltpu.VMEM((NZ - 1, NX, NY) + TILE, F32),
        pltpu.VMEM((NX - 1, NY) + TILE, F32),
        pltpu.VMEM((NY - 1, NX, NZ) + TILE, F32),
        pltpu.VMEM((NX - 1, NZ) + TILE, F32),
        pltpu.VMEM((NZ - 1,) + TILE, F32),
        pltpu.VMEM((2, NY, slots) + TILE, F32),
        pltpu.VMEM((NM * NX * NZ, 1, 128), F32),
        pltpu.VMEM((NLINE, 1, 128), F32),
        dma((11,)), pltpu.SemaphoreType.REGULAR((3,)),
        dma((slots,)), dma((slots,)),
        dma((2, 6)), dma((2, 6)),
        dma((2, NZ - 1)), dma((2, NZ - 1)),
        dma((2, NY - 1)), dma((2, NY - 1)),
        dma((NZ - 1,)), dma((NZ - 1,)),
        dma((NX - 1,)), dma((NX - 1,)),
        dma((NY - 1,)), dma((NY - 1,)),
        dma((NX - 1,)), dma((NX - 1,)),
        dma((NZ - 1,)), dma((NZ - 1,)),
        dma((NLINE - 1,)), dma((NLINE - 1,)),
        dma((NM * NX * NZ - 1,)), dma((NM * NX * NZ - 1,)),
        dma((NLINE - 1,)), dma((NLINE - 1,)),
    ]
    shapes = (
        jax.ShapeDtypeStruct((1, hidden // (NX * NZ), block), F32),
        jax.ShapeDtypeStruct((1, rows, hidden), BF16),
    )
    vmem = pl.BlockSpec(memory_space=pltpu.VMEM)
    anywhere = pl.BlockSpec(memory_space=pl.ANY)
    held = [pltpu.with_memory_space_constraint(v, pltpu.HBM) for v in (act, dy, w_out)]
    clipped, back = pl.pallas_call(
        functools.partial(kernel, float(entries)),
        out_shape=shapes,
        in_specs=[pl.BlockSpec(memory_space=pltpu.SMEM)] + [anywhere] * 3,
        out_specs=(vmem, vmem),
        scratch_shapes=scratch,
        compiler_params=pltpu.CompilerParams(
            collective_id=0, has_side_effects=True, vmem_limit_bytes=48 * 1024 * 1024
        ),
        name="grad_reduce",
    )(counts, *held)
    return pl.pallas_call(
        store,
        out_shape=shapes,
        in_specs=[vmem, vmem],
        out_specs=(anywhere, anywhere),
        scratch_shapes=[dma((2,))],
        name="store",
    )(*[pltpu.with_memory_space_constraint(v, pltpu.VMEM) for v in (clipped, back)])


def solution(mesh):
    in_specs = (
        P("mod", ("loop", "line"), None),
        P("mod", ("loop", "line"), None),
        P("mod", None, None),
        P("mod", "loop", "line"),
    )
    out_specs = (P("mod", "loop", None), P("mod", ("loop", "line"), None))
    return jax.shard_map(
        on_device, mesh=mesh, in_specs=in_specs, out_specs=out_specs, check_vma=False
    )
```

```python
import functools

import jax
import jax.numpy as jnp
from jax import lax
from jax.experimental import pallas as pl
from jax.experimental.pallas import tpu as pltpu
from jax.sharding import PartitionSpec as P

MESH = pl.DeviceIdType.MESH
F32 = jnp.float32
BF16 = jnp.bfloat16

NX, NZ, NY, NM = 4, 4, 8, 2
NLINE = NY * 2
COLS = 256
UNITS = ((0, 1, 2), (3, 4))
TILE = (8, 128)


def remote(src, dst, ssem, rsem, peer):
    return pltpu.make_async_remote_copy(
        src_ref=src, dst_ref=dst, send_sem=ssem, recv_sem=rsem, device_id=peer, device_id_type=MESH
    )


def settle(ref, sem):
    pltpu.make_async_copy(ref, ref, sem).wait()


def kernel(
    entries,
    cnt, act_hbm, dy_hbm, w_hbm,
    out_ref, hid_ref,
    act_v, dy_v, w_v, hid_v, act_t,
    pair_s, pair_r, own, xb, zr, yr,
    zr1, xr2, yrel, yr1, xr3, zr3,
    ag, s1, s2,
    act_sem, dy_sem, w_sem, hid_sem, gossip,
    pair_ss, pair_rs, x_ss, x_rs, z_ss, z_rs, y_ss, y_rs,
    zr1_ss, zr1_rs, xr2_ss, xr2_rs, yrel_ss, yrel_rs, yr1_ss, yr1_rs, xr3_ss, xr3_rs, zr3_ss, zr3_rs,
    ag_ss, ag_rs, s1_ss, s1_rs, s2_ss, s2_rs,
):
    mod = lax.axis_index("mod")
    loop = lax.axis_index("loop")
    line = lax.axis_index("line")
    x, z = loop // NZ, lax.rem(loop, NZ)
    y, core = line // 2, lax.rem(line, 2)
    rows, hidden = act_v.shape
    third = rows // 3

    def at(dm=0, dx=0, dz=0, dline=0):
        m2 = lax.rem(mod + dm, NM) if dm else mod
        x2 = lax.rem(x + dx, NX) if dx else x
        z2 = lax.rem(z + dz, NZ) if dz else z
        l2 = lax.rem(line + dline, NLINE) if dline else line
        return (m2, x2 * NZ + z2, l2)

    def along_z(d):
        ring = lax.rem(mod * NZ + z + d, NM * NZ)
        return (ring // NZ, x * NZ + lax.rem(ring, NZ), line)

    partner = (mod, loop, y * 2 + (1 - core))
    near_x = [at(dx=1), at(dx=NX - 1)]
    near_yz = [at(dline=2), at(dline=NLINE - 2), along_z(1), along_z(NM * NZ - 1)]

    def tell(r):
        for peer in (near_x + near_yz if r == 0 else near_yz):
            pl.semaphore_signal(gossip.at[r], inc=1, device_id=peer, device_id_type=MESH)

    def hear(r):
        pl.semaphore_wait(gossip.at[r], 6 if r == 0 else 4)

    right, left = lax.rem(x + 1, NX), lax.rem(x + 3, NX)
    across = lax.rem(x + 2, NX)
    lo, hi = pl.ds(0, 4), pl.ds(4, 4)

    def send(src, dst, ssem, rsem, peer):
        remote(src, dst, ssem, rsem, peer).start()

    def x_send(k, i):
        src, dx = (
            (own.at[k, across, :, lo], 1),
            (own.at[k, across, :, hi], 3),
            (own.at[k, right, :, hi], 1),
            (own.at[k, left, :, lo], 3),
            (own.at[k, right, :, lo], 1),
            (own.at[k, left, :, hi], 3),
        )[i]
        send(src, xb.at[k, i], x_ss.at[k], x_rs.at[k, min(i, 2)], at(dx=dx))

    def run(c):
        mine, theirs = UNITS[c], UNITS[1 - c]
        finish = []

        order = (3, 0, 4, 2, 1) if c == 0 else (0, 3, 2, 4, 1)
        load_act = []
        for i in range(6):
            part = pl.ds(i * (rows // 6), rows // 6)
            load_act.append(
                pltpu.make_async_copy(act_hbm.at[0, part], act_v.at[part], act_sem.at[i])
            )
            load_act[i].start()
        load_dy = {}
        for u in order:
            src = dy_hbm.at[0, :, pl.ds(u * COLS, COLS)]
            load_dy[u] = pltpu.make_async_copy(src, dy_v.at[u], dy_sem.at[u])
            load_dy[u].start()

        barrier = pltpu.get_barrier_semaphore()
        for peer in [partner] + near_x + near_yz:
            pl.semaphore_signal(barrier, inc=1, device_id=peer, device_id_type=MESH)

        count = cnt[0, 0, 0]
        for i in range(3):
            load_act[2 * i].wait()
            load_act[2 * i + 1].wait()
            flipped = act_v[i * third:(i + 1) * third, :].T
            alive = lax.broadcasted_iota(jnp.int32, (hidden, third), 1) + i * third < count
            act_t[:, i * third:(i + 1) * third] = jnp.where(alive, flipped, jnp.zeros_like(flipped))

        def product(u):
            load_dy[u].wait()
            dst = own.at[mine.index(u)] if u in mine else pair_s.at[theirs.index(u)]
            half = hidden // 2
            for i in range(2):
                acc = jnp.dot(
                    act_t[i * half:(i + 1) * half, :], dy_v[u], preferred_element_type=F32
                )
                tiles = acc.reshape(NX // 2, NZ, 4, 8, COLS)
                dst[2 * i:2 * i + 2, :, 0:4] = tiles[..., 0:128]
                dst[2 * i:2 * i + 2, :, 4:8] = tiles[..., 128:256]

        def send_pair(k):
            if theirs[k] in (2, 4):
                send(pair_s.at[k], pair_r.at[k], pair_ss.at[k], pair_rs.at[k, 0], partner)
            else:
                for d in (2, 1, 3, 0):
                    to = lax.rem(x + d, NX)
                    send(pair_s.at[k, to], pair_r.at[k, to], pair_ss.at[k], pair_rs.at[k, d], partner)
            finish.append((pair_s.at[k], pair_ss.at[k]))

        def hidden_rows(i):
            if i == 0:
                settle(w_v, w_sem)
            back = jnp.zeros((third, hidden), F32)
            for u in range(5):
                back = back + lax.dot_general(
                    dy_v[u, i * third:(i + 1) * third, :], w_v[u], (((1,), (1,)), ((), ())),
                    preferred_element_type=F32,
                )
            keep = lax.broadcasted_iota(jnp.int32, (third, hidden), 0) + i * third < count
            back = jnp.where(keep, back, jnp.zeros_like(back))
            hid_v[i * third:(i + 1) * third, :] = back.astype(BF16)
            part = pl.ds(i * third, third)
            pltpu.make_async_copy(hid_v.at[part], hid_ref.at[0, part], hid_sem).start()

        def merge_x(k, d):
            to = lax.rem(x + d, NX)
            settle(pair_r.at[k, to], pair_rs.at[k, d])
            own[k, to] = own[k, to] + pair_r[k, to]

        def e2(k):
            merge_x(k, 2)
            x_send(k, 0)
            x_send(k, 1)
            merge_x(k, 1)
            x_send(k, 2)
            merge_x(k, 3)
            x_send(k, 3)
            merge_x(k, 0)

        def e3(k):
            settle(xb.at[k, 0], x_rs.at[k, 0])
            own[k, right, :, 0:4] = own[k, right, :, 0:4] + xb[k, 0]
            x_send(k, 4)
            settle(xb.at[k, 1], x_rs.at[k, 1])
            own[k, left, :, 4:8] = own[k, left, :, 4:8] + xb[k, 1]
            x_send(k, 5)
            finish.append((xb.at[k], x_ss.at[k]))

        def e4(k):
            settle(xb.at[k, pl.ds(2, 4)], x_rs.at[k, 2])
            own[k, x, :, 0:4] = own[k, x, :, 0:4] + xb[k, 3] + xb[k, 4]
            own[k, x, :, 4:8] = own[k, x, :, 4:8] + xb[k, 2] + xb[k, 5]
            for d in (2, 1, 3):
                src = own.at[k, x, lax.rem(z + d, NZ)]
                send(src, zr.at[k, d - 1], z_ss.at[k], z_rs.at[k], at(dz=d))
            finish.append((zr.at[k], z_ss.at[k]))

        def to_y(k):
            for d in (4, 3, 5, 2, 6, 1, 7):
                src = own.at[k, x, z, lax.rem(y + d, NY)]
                send(src, yr.at[k, d - 1], y_ss.at[k], y_rs.at[k], at(dline=2 * d))
            finish.append((yr.at[k], y_ss.at[k]))

        def e5(k):
            settle(zr.at[k], z_rs.at[k])
            own[k, x, z] = own[k, x, z] + zr[k, 0] + zr[k, 1] + zr[k, 2]
            to_y(k)

        def e6(k):
            settle(yr.at[k], y_rs.at[k])
            total = own[k, x, z, y]
            for d in range(1, NY):
                total = total + yr[k, d - 1]
            ag[line, k] = total

        def a1(k):
            settle(pair_r.at[k], pair_rs.at[k, 0])
            for d in (2, 1, 3, 0):
                to = lax.rem(z + d, NZ)
                own[k, :, to] = own[k, :, to] + pair_r[k, :, to]
                if d:
                    send(own.at[k, :, to], zr1.at[d - 1], zr1_ss.at[0], zr1_rs.at[0], at(dz=d))
            finish.append((zr1, zr1_ss.at[0]))

        def a2(k):
            settle(zr1, zr1_rs.at[0])
            own[k, :, z] = own[k, :, z] + zr1[0] + zr1[1] + zr1[2]
            for d in (2, 1, 3):
                src = own.at[k, lax.rem(x + d, NX), z]
                send(src, xr2.at[d - 1], xr2_ss.at[0], xr2_rs.at[0], at(dx=d))
            finish.append((xr2, xr2_ss.at[0]))

        def a3(k):
            settle(xr2, xr2_rs.at[0])
            own[k, x, z] = own[k, x, z] + xr2[0] + xr2[1] + xr2[2]
            to_y(k)

        slot_of = {3: 0, 2: 1, 6: 2, 1: 3, 7: 4, 5: 5}

        def y_send(k, d):
            src = own.at[k, :, :, lax.rem(y + d, NY)]
            send(src, yr1.at[slot_of[d]], yr1_ss.at[0], yr1_rs.at[0], at(dline=2 * d))

        def b1(k):
            settle(pair_r.at[k], pair_rs.at[k, 0])
            for d in (4, 3, 2, 6, 1, 7, 5, 0):
                to = lax.rem(y + d, NY)
                own[k, :, :, to] = own[k, :, :, to] + pair_r[k, :, :, to]
                if d == 4:
                    send(own.at[k, :, :, to], yrel, yrel_ss.at[0], yrel_rs.at[0], at(dline=NLINE - 2))
                elif d in (3, 2, 6, 1, 7):
                    y_send(k, d)
            finish.append((yrel, yrel_ss.at[0]))

        def relay_y(k):
            settle(yrel, yrel_rs.at[0])
            to = lax.rem(y + 5, NY)
            own[k, :, :, to] = own[k, :, :, to] + yrel[...]
            y_send(k, 5)
            finish.append((yr1, yr1_ss.at[0]))

        def b2(k):
            settle(yr1, yr1_rs.at[0])
            total = own[k, :, :, y]
            for i in range(6):
                total = total + yr1[i]
            own[k, :, :, y] = total
            for d in (2, 1, 3):
                src = own.at[k, lax.rem(x + d, NX), :, y]
                send(src, xr3.at[d - 1], xr3_ss.at[0], xr3_rs.at[0], at(dx=d))
            finish.append((xr3, xr3_ss.at[0]))

        def b3(k):
            settle(xr3, xr3_rs.at[0])
            own[k, x, :, y] = own[k, x, :, y] + xr3[0] + xr3[1] + xr3[2]
            for d in (2, 1, 3):
                src = own.at[k, x, lax.rem(z + d, NZ), y]
                send(src, zr3.at[d - 1], zr3_ss.at[0], zr3_rs.at[0], at(dz=d))
            finish.append((zr3, zr3_ss.at[0]))

        def b4(k):
            settle(zr3, zr3_rs.at[0])
            ag[line, k] = own[k, x, z, y] + zr3[0] + zr3[1] + zr3[2]

        product(order[0])
        pl.semaphore_wait(barrier, 7)
        tell(0)
        send_pair(0)
        for u in range(5):
            src = w_hbm.at[0, :, pl.ds(u * COLS, COLS)]
            pltpu.make_async_copy(src, w_v.at[u], w_sem).start()
        product(order[1])
        product(order[2])
        send_pair(1 if c == 0 else 2)
        hear(0)
        tell(1)
        e2(0)
        product(order[3])
        product(order[4])
        if c == 1:
            send_pair(1)
        hear(1)
        tell(2)
        if c == 0:
            b1(2)
            e2(1)
            e3(0)
            hidden_rows(0)
            relay_y(2)
            e3(1)
            hidden_rows(1)
            hear(2)
            e4(0)
            hidden_rows(2)
            e4(1)
            e5(0)
            b2(2)
            e5(1)
            b3(2)
            e6(0)
            e6(1)
            b4(2)
        else:
            ag[line, 2] = jnp.zeros(TILE, F32)
            a1(1)
            e3(0)
            hidden_rows(0)
            hidden_rows(1)
            hear(2)
            hidden_rows(2)
            e4(0)
            a2(1)
            e5(0)
            a3(1)
            e6(0)
            e6(1)
        for ref, sem in finish:
            settle(ref, sem)
        settle(hid_v, hid_sem)

    pl.when(core == 0)(functools.partial(run, 0))
    pl.when(core == 1)(functools.partial(run, 1))

    offsets = [(dm, dx, dz) for dm in range(NM) for dx in range(NX) for dz in range(NZ)][1:]
    shard = ag[line]
    s1[0] = jnp.sum(jnp.sum(shard * shard, axis=0), axis=0, keepdims=True)
    for i, offset in enumerate(offsets):
        send(s1.at[0], s1.at[i + 1], s1_ss.at[0], s1_rs.at[0], at(*offset))
    for d in range(1, NLINE):
        send(ag.at[line], ag.at[line], ag_ss.at[0], ag_rs.at[0], at(dline=d))
    rest1, rest2, rest3 = s1.at[pl.ds(1, len(offsets))], s2.at[pl.ds(1, NLINE - 1)], ag.at[pl.ds(0, NLINE - 1)]
    settle(rest1, s1_rs.at[0])
    s2[0] = jnp.sum(s1[...], axis=0)
    for d in range(1, NLINE):
        send(s2.at[0], s2.at[d], s2_ss.at[0], s2_rs.at[0], at(dline=d))
    settle(rest1, s1_ss.at[0])
    settle(rest3, ag_rs.at[0])
    settle(rest3, ag_ss.at[0])
    settle(rest2, s2_rs.at[0])
    total = jnp.sum(jnp.sum(s2[...], axis=0), axis=-1, keepdims=True)
    factor = 1.0 / jnp.sqrt(total / entries + 1e-06)
    for c in range(2):
        for k, u in enumerate(UNITS[c]):
            for q in range(NY):
                r, col = (q % 4) * 8, u * COLS + (q // 4) * 128
                out_ref[0, r:r + 8, col:col + 128] = ag[q * 2 + c, k] * factor
    settle(rest2, s2_ss.at[0])


def store(a_ref, b_ref, a_out, b_out, sem):
    n = b_ref.shape[1] // 8
    copies = [pltpu.make_async_copy(a_ref, a_out, sem.at[8])]
    for i in range(8):
        part = pl.ds(i * n, n)
        copies.append(pltpu.make_async_copy(b_ref.at[0, part], b_out.at[0, part], sem.at[i]))
    for copy in copies:
        copy.start()
    for copy in copies:
        copy.wait()


def on_device(act, dy, w_out, counts):
    rows, hidden = act.shape[1:]
    block = w_out.shape[2]
    entries = NM * hidden * block
    dma = pltpu.SemaphoreType.DMA
    slots = 3
    unit = (NX, NZ, NY) + TILE
    scratch = [
        pltpu.VMEM((rows, hidden), BF16),
        pltpu.VMEM((5, rows, COLS), BF16),
        pltpu.VMEM((5, hidden, COLS), BF16),
        pltpu.VMEM((rows, hidden), BF16),
        pltpu.VMEM((hidden, rows), BF16),
        pltpu.VMEM((slots,) + unit, F32),
        pltpu.VMEM((slots,) + unit, F32),
        pltpu.VMEM((slots,) + unit, F32),
        pltpu.VMEM((2, 6, NZ, 4) + TILE, F32),
        pltpu.VMEM((2, NZ - 1, NY) + TILE, F32),
        pltpu.VMEM((2, NY - 1) + TILE, F32),
        pltpu.VMEM((NZ - 1, NX, NY) + TILE, F32),
        pltpu.VMEM((NX - 1, NY) + TILE, F32),
        pltpu.VMEM((NX, NZ) + TILE, F32),
        pltpu.VMEM((NY - 2, NX, NZ) + TILE, F32),
        pltpu.VMEM((NX - 1, NZ) + TILE, F32),
        pltpu.VMEM((NZ - 1,) + TILE, F32),
        pltpu.VMEM((NLINE, slots) + TILE, F32),
        pltpu.VMEM((NM * NX * NZ, 1, 128), F32),
        pltpu.VMEM((NLINE, 1, 128), F32),
        dma((6,)), dma((5,)), dma(()), dma(()), pltpu.SemaphoreType.REGULAR((3,)),
        dma((slots,)), dma((slots, 4)),
        dma((2,)), dma((2, 3)),
        dma((2,)), dma((2,)), dma((2,)), dma((2,)),
    ] + [dma((1,))] * 18
    shapes = (
        jax.ShapeDtypeStruct((1, hidden // (NX * NZ), block), F32),
        jax.ShapeDtypeStruct((1, rows, hidden), BF16),
    )
    vmem = pl.BlockSpec(memory_space=pltpu.VMEM)
    anywhere = pl.BlockSpec(memory_space=pl.ANY)
    held = [pltpu.with_memory_space_constraint(v, pltpu.HBM) for v in (act, dy, w_out)]
    clipped, back = pl.pallas_call(
        functools.partial(kernel, float(entries)),
        out_shape=shapes,
        in_specs=[pl.BlockSpec(memory_space=pltpu.SMEM)] + [anywhere] * 3,
        out_specs=(vmem, anywhere),
        scratch_shapes=scratch,
        compiler_params=pltpu.CompilerParams(
            collective_id=0, has_side_effects=True, vmem_limit_bytes=48 * 1024 * 1024
        ),
        name="grad_reduce",
    )(counts, *held)
    return pl.pallas_call(
        store,
        out_shape=shapes,
        in_specs=[vmem, vmem],
        out_specs=(anywhere, anywhere),
        scratch_shapes=[dma((9,))],
        name="store",
    )(*[pltpu.with_memory_space_constraint(v, pltpu.VMEM) for v in (clipped, back)])


def solution(mesh):
    in_specs = (
        P("mod", ("loop", "line"), None),
        P("mod", ("loop", "line"), None),
        P("mod", None, None),
        P("mod", "loop", "line"),
    )
    out_specs = (P("mod", "loop", None), P("mod", ("loop", "line"), None))
    return jax.shard_map(
        on_device, mesh=mesh, in_specs=in_specs, out_specs=out_specs, check_vma=False
    )
```

```python
import functools

import jax
import jax.numpy as jnp
from jax import lax
from jax.experimental import pallas as pl
from jax.experimental.pallas import tpu as pltpu
from jax.sharding import PartitionSpec as P

MESH = pl.DeviceIdType.MESH
F32 = jnp.float32
BF16 = jnp.bfloat16

NX, NZ, NY, NM = 4, 4, 8, 2
NLINE = NY * 2
COLS = 256
UNITS = ((0, 1, 2), (3, 4))
TILE = (8, 128)
Y_THEN_Z = (0, 1)


def remote(src, dst, ssem, rsem, peer):
    return pltpu.make_async_remote_copy(
        src_ref=src, dst_ref=dst, send_sem=ssem, recv_sem=rsem, device_id=peer, device_id_type=MESH
    )


def settle(ref, sem):
    pltpu.make_async_copy(ref, ref, sem).wait()


def kernel(
    entries,
    cnt, act_hbm, dy_hbm, w_hbm,
    out_ref, hid_ref,
    act_v, dy_v, w_v, hid_v, act_t,
    pair_s, pair_r, own, xb, zr, yz, yzz, yr,
    zr1, xr2, yrel, yr1, xr3, zr3,
    ag, s1, s2,
    act_sem, dy_sem, w_sem, hid_sem, gossip,
    pair_ss, pair_rs, x_ss, x_rs, z_ss, z_rs, yz_ss, yz_rs, y_ss, y_rs,
    zr1_ss, zr1_rs, xr2_ss, xr2_rs, yrel_ss, yrel_rs, yr1_ss, yr1_rs, xr3_ss, xr3_rs, zr3_ss, zr3_rs,
    ag_ss, ag_rs, s1_ss, s1_rs, s2_ss, s2_rs,
):
    mod = lax.axis_index("mod")
    loop = lax.axis_index("loop")
    line = lax.axis_index("line")
    x, z = loop // NZ, lax.rem(loop, NZ)
    y, core = line // 2, lax.rem(line, 2)
    rows, hidden = act_v.shape
    third = rows // 3

    def at(dm=0, dx=0, dz=0, dline=0):
        m2 = lax.rem(mod + dm, NM) if dm else mod
        x2 = lax.rem(x + dx, NX) if dx else x
        z2 = lax.rem(z + dz, NZ) if dz else z
        l2 = lax.rem(line + dline, NLINE) if dline else line
        return (m2, x2 * NZ + z2, l2)

    def along_z(d):
        ring = lax.rem(mod * NZ + z + d, NM * NZ)
        return (ring // NZ, x * NZ + lax.rem(ring, NZ), line)

    partner = (mod, loop, y * 2 + (1 - core))
    near_x = [at(dx=1), at(dx=NX - 1)]
    near_yz = [at(dline=2), at(dline=NLINE - 2), along_z(1), along_z(NM * NZ - 1)]

    def tell(r):
        for peer in (near_x + near_yz if r == 0 else near_yz):
            pl.semaphore_signal(gossip.at[r], inc=1, device_id=peer, device_id_type=MESH)

    def hear(r):
        pl.semaphore_wait(gossip.at[r], 6 if r == 0 else 4)

    right, left = lax.rem(x + 1, NX), lax.rem(x + 3, NX)
    across = lax.rem(x + 2, NX)
    lo, hi = pl.ds(0, 4), pl.ds(4, 4)

    def send(src, dst, ssem, rsem, peer):
        remote(src, dst, ssem, rsem, peer).start()

    def x_send(k, i):
        src, dx = (
            (own.at[k, across, :, lo], 1),
            (own.at[k, across, :, hi], 3),
            (own.at[k, right, :, hi], 1),
            (own.at[k, left, :, lo], 3),
            (own.at[k, right, :, lo], 1),
            (own.at[k, left, :, hi], 3),
        )[i]
        send(src, xb.at[k, i], x_ss.at[k], x_rs.at[k, min(i, 2)], at(dx=dx))

    count = cnt[0, 0, 0]

    def hidden_rows(i):
        back = jnp.zeros((third, hidden), F32)
        for u in range(5):
            back = back + lax.dot_general(
                dy_v[u, i * third:(i + 1) * third, :], w_v[u], (((1,), (1,)), ((), ())),
                preferred_element_type=F32,
            )
        keep = lax.broadcasted_iota(jnp.int32, (third, hidden), 0) + i * third < count
        back = jnp.where(keep, back, jnp.zeros_like(back))
        hid_v[i * third:(i + 1) * third, :] = back.astype(BF16)
        part = pl.ds(i * third, third)
        pltpu.make_async_copy(hid_v.at[part], hid_ref.at[0, part], hid_sem).start()

    def run(c):
        mine, theirs = UNITS[c], UNITS[1 - c]
        finish = []

        order = (3, 0, 4, 2, 1) if c == 0 else (0, 3, 2, 4, 1)
        load_act = []
        for i in range(6):
            part = pl.ds(i * (rows // 6), rows // 6)
            load_act.append(
                pltpu.make_async_copy(act_hbm.at[0, part], act_v.at[part], act_sem.at[i])
            )
            load_act[i].start()
        load_dy = {}
        for u in order:
            src = dy_hbm.at[0, :, pl.ds(u * COLS, COLS)]
            load_dy[u] = pltpu.make_async_copy(src, dy_v.at[u], dy_sem.at[u])
        load_dy[order[0]].start()
        load_dy[order[1]].start()

        barrier = pltpu.get_barrier_semaphore()
        for peer in [partner] + near_x + near_yz:
            pl.semaphore_signal(barrier, inc=1, device_id=peer, device_id_type=MESH)

        for i in range(3):
            load_act[2 * i].wait()
            load_act[2 * i + 1].wait()
            flipped = act_v[i * third:(i + 1) * third, :].T
            alive = lax.broadcasted_iota(jnp.int32, (hidden, third), 1) + i * third < count
            act_t[:, i * third:(i + 1) * third] = jnp.where(alive, flipped, jnp.zeros_like(flipped))

        for u in order[2:]:
            load_dy[u].start()

        def product(u):
            load_dy[u].wait()
            dst = own.at[mine.index(u)] if u in mine else pair_s.at[theirs.index(u)]
            half = hidden // 2
            for i in range(2):
                acc = jnp.dot(
                    act_t[i * half:(i + 1) * half, :], dy_v[u], preferred_element_type=F32
                )
                tiles = acc.reshape(NX // 2, NZ, 4, 8, COLS)
                dst[2 * i:2 * i + 2, :, 0:4] = tiles[..., 0:128]
                dst[2 * i:2 * i + 2, :, 4:8] = tiles[..., 128:256]

        late = 1 if c == 0 else 2

        def send_pair(k):
            if theirs[k] in (2, 4):
                send(pair_s.at[k], pair_r.at[k], pair_ss.at[k], pair_rs.at[k, 0], partner)
            else:
                for d in (2, 1, 3) if k == 0 else (2, 1, 3, 0):
                    to = lax.rem(x + d, NX)
                    send(pair_s.at[k, to], pair_r.at[k, to], pair_ss.at[k], pair_rs.at[k, d], partner)
            if k == late:
                send(pair_s.at[0, x], pair_r.at[0, x], pair_ss.at[0], pair_rs.at[0, 0], partner)
            finish.append((pair_s.at[k], pair_ss.at[k]))

        def merge_x(k, d):
            to = lax.rem(x + d, NX)
            settle(pair_r.at[k, to], pair_rs.at[k, d])
            own[k, to] = own[k, to] + pair_r[k, to]

        def e2(k):
            merge_x(k, 2)
            x_send(k, 0)
            x_send(k, 1)
            merge_x(k, 1)
            x_send(k, 2)
            merge_x(k, 3)
            x_send(k, 3)

        def e3(k):
            settle(xb.at[k, 0], x_rs.at[k, 0])
            own[k, right, :, 0:4] = own[k, right, :, 0:4] + xb[k, 0]
            x_send(k, 4)
            settle(xb.at[k, 1], x_rs.at[k, 1])
            own[k, left, :, 4:8] = own[k, left, :, 4:8] + xb[k, 1]
            x_send(k, 5)
            finish.append((xb.at[k], x_ss.at[k]))

        def e4(k):
            merge_x(k, 0)
            settle(xb.at[k, pl.ds(2, 4)], x_rs.at[k, 2])
            own[k, x, :, 0:4] = own[k, x, :, 0:4] + xb[k, 3] + xb[k, 4]
            own[k, x, :, 4:8] = own[k, x, :, 4:8] + xb[k, 2] + xb[k, 5]
            if k in Y_THEN_Z:
                for d in (4, 3, 5, 2, 6, 1, 7):
                    src = own.at[k, x, :, lax.rem(y + d, NY)]
                    send(src, yz.at[k, d - 1], yz_ss.at[k], yz_rs.at[k], at(dline=2 * d))
                finish.append((yz.at[k], yz_ss.at[k]))
                return
            for d in (2, 1, 3):
                src = own.at[k, x, lax.rem(z + d, NZ)]
                send(src, zr.at[k, d - 1], z_ss.at[k], z_rs.at[k], at(dz=d))
            finish.append((zr.at[k], z_ss.at[k]))

        def to_y(k):
            for d in (4, 3, 5, 2, 6, 1, 7):
                src = own.at[k, x, z, lax.rem(y + d, NY)]
                send(src, yr.at[k, d - 1], y_ss.at[k], y_rs.at[k], at(dline=2 * d))
            finish.append((yr.at[k], y_ss.at[k]))

        def e5(k):
            if k in Y_THEN_Z:
                settle(yz.at[k], yz_rs.at[k])
                total = own[k, x, :, y]
                for d in range(1, NY):
                    total = total + yz[k, d - 1]
                own[k, x, :, y] = total
                for d in (2, 1, 3):
                    src = own.at[k, x, lax.rem(z + d, NZ), y]
                    send(src, yzz.at[k, d - 1], z_ss.at[k], z_rs.at[k], at(dz=d))
                finish.append((yzz.at[k], z_ss.at[k]))
                return
            settle(zr.at[k], z_rs.at[k])
            own[k, x, z] = own[k, x, z] + zr[k, 0] + zr[k, 1] + zr[k, 2]
            to_y(k)

        def e6(k):
            if k in Y_THEN_Z and (c, k) != (1, 1):
                settle(yzz.at[k], z_rs.at[k])
                ag[line, k] = own[k, x, z, y] + yzz[k, 0] + yzz[k, 1] + yzz[k, 2]
                return
            settle(yr.at[k], y_rs.at[k])
            total = own[k, x, z, y]
            for d in range(1, NY):
                total = total + yr[k, d - 1]
            ag[line, k] = total

        def a1(k):
            settle(pair_r.at[k], pair_rs.at[k, 0])
            for d in (2, 1, 3, 0):
                to = lax.rem(z + d, NZ)
                own[k, :, to] = own[k, :, to] + pair_r[k, :, to]
                if d:
                    send(own.at[k, :, to], zr1.at[d - 1], zr1_ss.at[0], zr1_rs.at[0], at(dz=d))
            finish.append((zr1, zr1_ss.at[0]))

        def a2(k):
            settle(zr1, zr1_rs.at[0])
            own[k, :, z] = own[k, :, z] + zr1[0] + zr1[1] + zr1[2]
            for d in (2, 1, 3):
                src = own.at[k, lax.rem(x + d, NX), z]
                send(src, xr2.at[d - 1], xr2_ss.at[0], xr2_rs.at[0], at(dx=d))
            finish.append((xr2, xr2_ss.at[0]))

        def a3(k):
            settle(xr2, xr2_rs.at[0])
            own[k, x, z] = own[k, x, z] + xr2[0] + xr2[1] + xr2[2]
            to_y(k)

        slot_of = {3: 0, 2: 1, 6: 2, 1: 3, 7: 4, 5: 5}

        def y_send(k, d):
            src = own.at[k, :, :, lax.rem(y + d, NY)]
            send(src, yr1.at[slot_of[d]], yr1_ss.at[0], yr1_rs.at[0], at(dline=2 * d))

        def b1(k):
            settle(pair_r.at[k], pair_rs.at[k, 0])
            for d in (4, 2, 6, 1, 7, 3, 5, 0):
                to = lax.rem(y + d, NY)
                own[k, :, :, to] = own[k, :, :, to] + pair_r[k, :, :, to]
                if d == 4:
                    send(own.at[k, :, :, to], yrel, yrel_ss.at[0], yrel_rs.at[0], at(dline=NLINE - 2))
                elif d in (2, 6, 1, 7):
                    y_send(k, d)
            finish.append((yrel, yrel_ss.at[0]))

        def relay_y(k):
            settle(yrel, yrel_rs.at[0])
            to = lax.rem(y + 5, NY)
            own[k, :, :, to] = own[k, :, :, to] + yrel[...]
            y_send(k, 5)
            finish.append((yr1, yr1_ss.at[0]))

        def b2(k):
            settle(yr1, yr1_rs.at[0])
            total = own[k, :, :, y]
            for i in range(6):
                total = total + yr1[i]
            own[k, :, :, y] = total
            for d in (2, 1, 3):
                src = own.at[k, lax.rem(x + d, NX), :, y]
                send(src, xr3.at[d - 1], xr3_ss.at[0], xr3_rs.at[0], at(dx=d))
            finish.append((xr3, xr3_ss.at[0]))

        def b3(k):
            settle(xr3, xr3_rs.at[0])
            own[k, x, :, y] = own[k, x, :, y] + xr3[0] + xr3[1] + xr3[2]
            for d in (2, 1, 3):
                src = own.at[k, x, lax.rem(z + d, NZ), y]
                send(src, zr3.at[d - 1], zr3_ss.at[0], zr3_rs.at[0], at(dz=d))
            finish.append((zr3, zr3_ss.at[0]))

        def b4(k):
            settle(zr3, zr3_rs.at[0])
            ag[line, k] = own[k, x, z, y] + zr3[0] + zr3[1] + zr3[2]

        product(order[0])
        pl.semaphore_wait(barrier, 7)
        tell(0)
        send_pair(0)
        for u in range(5):
            src = w_hbm.at[0, :, pl.ds(u * COLS, COLS)]
            pltpu.make_async_copy(src, w_v.at[u], w_sem).start()
        product(order[1])
        product(order[2])
        send_pair(1 if c == 0 else 2)
        e2(0)
        hear(0)
        tell(1)
        product(order[3])
        product(order[4])
        if c == 0:
            b1(2)
            e2(1)
        else:
            send_pair(1)
        hear(1)
        tell(2)
        if c == 0:
            y_send(2, 3)
            e3(0)
            relay_y(2)
            e3(1)
            hear(2)
            e4(0)
            e4(1)
            b2(2)
            e5(0)
            b3(2)
            e5(1)
            b4(2)
            e6(0)
            e6(1)
        else:
            ag[line, 2] = jnp.zeros(TILE, F32)
            a1(1)
            e3(0)
            hear(2)
            e4(0)
            a2(1)
            e5(0)
            a3(1)
            e6(0)
            e6(1)
        for ref, sem in finish:
            settle(ref, sem)

    pl.when(core == 0)(functools.partial(run, 0))
    pl.when(core == 1)(functools.partial(run, 1))

    offsets = [(dm, dx, dz) for dm in range(NM) for dx in range(NX) for dz in range(NZ)][:0:-1]
    shard = ag[line]
    s1[0] = jnp.sum(jnp.sum(shard * shard, axis=0), axis=0, keepdims=True)
    for i, offset in enumerate(offsets):
        send(s1.at[0], s1.at[i + 1], s1_ss.at[0], s1_rs.at[0], at(*offset))
    for d in range(1, NLINE):
        send(ag.at[line], ag.at[line], ag_ss.at[0], ag_rs.at[0], at(dline=d))
    rest1, rest2, rest3 = s1.at[pl.ds(1, len(offsets))], s2.at[pl.ds(1, NLINE - 1)], ag.at[pl.ds(0, NLINE - 1)]
    settle(w_v, w_sem)
    for i in range(3):
        hidden_rows(i)
    settle(rest1, s1_rs.at[0])
    s2[0] = jnp.sum(s1[...], axis=0)
    for d in range(1, NLINE):
        send(s2.at[0], s2.at[d], s2_ss.at[0], s2_rs.at[0], at(dline=d))
    settle(rest1, s1_ss.at[0])
    settle(rest3, ag_rs.at[0])
    settle(rest3, ag_ss.at[0])
    settle(rest2, s2_rs.at[0])
    total = jnp.sum(jnp.sum(s2[...], axis=0), axis=-1, keepdims=True)
    factor = 1.0 / jnp.sqrt(total / entries + 1e-06)
    for c in range(2):
        for k, u in enumerate(UNITS[c]):
            for q in range(NY):
                r, col = (q % 4) * 8, u * COLS + (q // 4) * 128
                out_ref[0, r:r + 8, col:col + 128] = ag[q * 2 + c, k] * factor
    settle(rest2, s2_ss.at[0])
    settle(hid_v, hid_sem)


def store(a_ref, b_ref, a_out, b_out, sem):
    n = b_ref.shape[1] // 2
    copies = [pltpu.make_async_copy(a_ref, a_out, sem.at[2])]
    for i in range(2):
        part = pl.ds(i * n, n)
        copies.append(pltpu.make_async_copy(b_ref.at[0, part], b_out.at[0, part], sem.at[i]))
    for copy in copies:
        copy.start()
    for copy in copies:
        copy.wait()


def on_device(act, dy, w_out, counts):
    rows, hidden = act.shape[1:]
    block = w_out.shape[2]
    entries = NM * hidden * block
    dma = pltpu.SemaphoreType.DMA
    slots = 3
    unit = (NX, NZ, NY) + TILE
    scratch = [
        pltpu.VMEM((rows, hidden), BF16),
        pltpu.VMEM((5, rows, COLS), BF16),
        pltpu.VMEM((5, hidden, COLS), BF16),
        pltpu.VMEM((rows, hidden), BF16),
        pltpu.VMEM((hidden, rows), BF16),
        pltpu.VMEM((slots,) + unit, F32),
        pltpu.VMEM((slots,) + unit, F32),
        pltpu.VMEM((slots,) + unit, F32),
        pltpu.VMEM((2, 6, NZ, 4) + TILE, F32),
        pltpu.VMEM((2, NZ - 1, NY) + TILE, F32),
        pltpu.VMEM((2, NY - 1, NZ) + TILE, F32),
        pltpu.VMEM((2, NZ - 1) + TILE, F32),
        pltpu.VMEM((2, NY - 1) + TILE, F32),
        pltpu.VMEM((NZ - 1, NX, NY) + TILE, F32),
        pltpu.VMEM((NX - 1, NY) + TILE, F32),
        pltpu.VMEM((NX, NZ) + TILE, F32),
        pltpu.VMEM((NY - 2, NX, NZ) + TILE, F32),
        pltpu.VMEM((NX - 1, NZ) + TILE, F32),
        pltpu.VMEM((NZ - 1,) + TILE, F32),
        pltpu.VMEM((NLINE, slots) + TILE, F32),
        pltpu.VMEM((NM * NX * NZ, 1, 128), F32),
        pltpu.VMEM((NLINE, 1, 128), F32),
        dma((6,)), dma((5,)), dma(()), dma(()), pltpu.SemaphoreType.REGULAR((3,)),
        dma((slots,)), dma((slots, 4)),
        dma((2,)), dma((2, 3)),
        dma((2,)), dma((2,)), dma((2,)), dma((2,)), dma((2,)), dma((2,)),
    ] + [dma((1,))] * 18
    shapes = (
        jax.ShapeDtypeStruct((1, hidden // (NX * NZ), block), F32),
        jax.ShapeDtypeStruct((1, rows, hidden), BF16),
    )
    vmem = pl.BlockSpec(memory_space=pltpu.VMEM)
    anywhere = pl.BlockSpec(memory_space=pl.ANY)
    held = [pltpu.with_memory_space_constraint(v, pltpu.HBM) for v in (act, dy, w_out)]
    clipped, back = pl.pallas_call(
        functools.partial(kernel, float(entries)),
        out_shape=shapes,
        in_specs=[pl.BlockSpec(memory_space=pltpu.SMEM)] + [anywhere] * 3,
        out_specs=(vmem, anywhere),
        scratch_shapes=scratch,
        compiler_params=pltpu.CompilerParams(
            collective_id=0, has_side_effects=True, vmem_limit_bytes=48 * 1024 * 1024
        ),
        name="grad_reduce",
    )(counts, *held)
    return pl.pallas_call(
        store,
        out_shape=shapes,
        in_specs=[vmem, vmem],
        out_specs=(anywhere, anywhere),
        scratch_shapes=[dma((3,))],
        name="store",
    )(*[pltpu.with_memory_space_constraint(v, pltpu.VMEM) for v in (clipped, back)])


def solution(mesh):
    in_specs = (
        P("mod", ("loop", "line"), None),
        P("mod", ("loop", "line"), None),
        P("mod", None, None),
        P("mod", "loop", "line"),
    )
    out_specs = (P("mod", "loop", None), P("mod", ("loop", "line"), None))
    return jax.shard_map(
        on_device, mesh=mesh, in_specs=in_specs, out_specs=out_specs, check_vma=False
    )
```

```python
import functools

import jax
import jax.numpy as jnp
from jax import lax
from jax.experimental import pallas as pl
from jax.experimental.pallas import tpu as pltpu
from jax.sharding import PartitionSpec as P

MESH = pl.DeviceIdType.MESH
F32 = jnp.float32
BF16 = jnp.bfloat16

NX, NZ, NY, NM = 4, 4, 8, 2
NLINE = NY * 2
COLS = 256
UNITS = ((0, 1, 2), (3, 4))
TILE = (8, 128)
Y_THEN_Z = ((1, 0), (0, 1))


def remote(src, dst, ssem, rsem, peer):
    return pltpu.make_async_remote_copy(
        src_ref=src, dst_ref=dst, send_sem=ssem, recv_sem=rsem, device_id=peer, device_id_type=MESH
    )


def settle(ref, sem):
    pltpu.make_async_copy(ref, ref, sem).wait()


def kernel(
    entries,
    cnt, act_hbm, dy_hbm, w_hbm,
    out_ref, hid_ref,
    act_v, dy_v, w_v, hid_v, act_t,
    pair_s, pair_r, own, xb, zr, yz, yzz, yr,
    zr1, xr2, yrel, yr1, xr3, zr3,
    ag, s1, s2,
    act_sem, dy_sem, w_sem, hid_sem, gossip,
    pair_ss, pair_rs, x_ss, x_rs, z_ss, z_rs, yz_ss, yz_rs, y_ss, y_rs,
    zr1_ss, zr1_rs, xr2_ss, xr2_rs, yrel_ss, yrel_rs, yr1_ss, yr1_rs, xr3_ss, xr3_rs, zr3_ss, zr3_rs,
    ag_ss, ag_rs, s1_ss, s1_rs, s2_ss, s2_rs,
):
    mod = lax.axis_index("mod")
    loop = lax.axis_index("loop")
    line = lax.axis_index("line")
    x, z = loop // NZ, lax.rem(loop, NZ)
    y, core = line // 2, lax.rem(line, 2)
    rows, hidden = act_v.shape
    third = rows // 3

    def at(dm=0, dx=0, dz=0, dline=0):
        m2 = lax.rem(mod + dm, NM) if dm else mod
        x2 = lax.rem(x + dx, NX) if dx else x
        z2 = lax.rem(z + dz, NZ) if dz else z
        l2 = lax.rem(line + dline, NLINE) if dline else line
        return (m2, x2 * NZ + z2, l2)

    def along_z(d):
        ring = lax.rem(mod * NZ + z + d, NM * NZ)
        return (ring // NZ, x * NZ + lax.rem(ring, NZ), line)

    partner = (mod, loop, y * 2 + (1 - core))
    near_x = [at(dx=1), at(dx=NX - 1)]
    near_yz = [at(dline=2), at(dline=NLINE - 2), along_z(1), along_z(NM * NZ - 1)]

    def tell(r):
        for peer in (near_x + near_yz if r == 0 else near_yz):
            pl.semaphore_signal(gossip.at[r], inc=1, device_id=peer, device_id_type=MESH)

    def hear(r):
        pl.semaphore_wait(gossip.at[r], 6 if r == 0 else 4)

    right, left = lax.rem(x + 1, NX), lax.rem(x + 3, NX)
    across = lax.rem(x + 2, NX)
    lo, hi = pl.ds(0, 4), pl.ds(4, 4)

    def send(src, dst, ssem, rsem, peer):
        remote(src, dst, ssem, rsem, peer).start()

    def x_send(k, i):
        src, dx = (
            (own.at[k, across, :, lo], 1),
            (own.at[k, across, :, hi], 3),
            (own.at[k, right, :, hi], 1),
            (own.at[k, left, :, lo], 3),
            (own.at[k, right, :, lo], 1),
            (own.at[k, left, :, hi], 3),
        )[i]
        send(src, xb.at[k, i], x_ss.at[k], x_rs.at[k, min(i, 2)], at(dx=dx))

    count = cnt[0, 0, 0]

    def hidden_rows(i):
        back = jnp.zeros((third, hidden), F32)
        for u in range(5):
            back = back + lax.dot_general(
                dy_v[u, i * third:(i + 1) * third, :], w_v[u], (((1,), (1,)), ((), ())),
                preferred_element_type=F32,
            )
        keep = lax.broadcasted_iota(jnp.int32, (third, hidden), 0) + i * third < count
        back = jnp.where(keep, back, jnp.zeros_like(back))
        hid_v[i * third:(i + 1) * third, :] = back.astype(BF16)
        part = pl.ds(i * third, third)
        pltpu.make_async_copy(hid_v.at[part], hid_ref.at[0, part], hid_sem).start()

    def run(c):
        mine, theirs = UNITS[c], UNITS[1 - c]
        finish = []

        order = (3, 0, 4, 2, 1) if c == 0 else (0, 3, 2, 4, 1)
        load_act = []
        for i in range(6):
            part = pl.ds(i * (rows // 6), rows // 6)
            load_act.append(
                pltpu.make_async_copy(act_hbm.at[0, part], act_v.at[part], act_sem.at[i])
            )
            load_act[i].start()
        load_dy = {}
        for u in order:
            src = dy_hbm.at[0, :, pl.ds(u * COLS, COLS)]
            load_dy[u] = pltpu.make_async_copy(src, dy_v.at[u], dy_sem.at[u])
        load_dy[order[0]].start()
        load_dy[order[1]].start()

        barrier = pltpu.get_barrier_semaphore()
        for peer in [partner] + near_x + near_yz:
            pl.semaphore_signal(barrier, inc=1, device_id=peer, device_id_type=MESH)

        for i in range(3):
            load_act[2 * i].wait()
            load_act[2 * i + 1].wait()
            flipped = act_v[i * third:(i + 1) * third, :].T
            alive = lax.broadcasted_iota(jnp.int32, (hidden, third), 1) + i * third < count
            act_t[:, i * third:(i + 1) * third] = jnp.where(alive, flipped, jnp.zeros_like(flipped))

        for u in order[2:]:
            load_dy[u].start()

        def product(u):
            load_dy[u].wait()
            dst = own.at[mine.index(u)] if u in mine else pair_s.at[theirs.index(u)]
            half = hidden // 2
            for i in range(2):
                acc = jnp.dot(
                    act_t[i * half:(i + 1) * half, :], dy_v[u], preferred_element_type=F32
                )
                tiles = acc.reshape(NX // 2, NZ, 4, 8, COLS)
                dst[2 * i:2 * i + 2, :, 0:4] = tiles[..., 0:128]
                dst[2 * i:2 * i + 2, :, 4:8] = tiles[..., 128:256]

        late = 1 if c == 0 else 2

        def send_pair(k):
            if theirs[k] in (2, 4):
                send(pair_s.at[k], pair_r.at[k], pair_ss.at[k], pair_rs.at[k, 0], partner)
            else:
                for d in (2, 1, 3) if k == 0 else (2, 1, 3, 0):
                    to = lax.rem(x + d, NX)
                    send(pair_s.at[k, to], pair_r.at[k, to], pair_ss.at[k], pair_rs.at[k, d], partner)
            if k == late:
                send(pair_s.at[0, x], pair_r.at[0, x], pair_ss.at[0], pair_rs.at[0, 0], partner)
            finish.append((pair_s.at[k], pair_ss.at[k]))

        def merge_x(k, d):
            to = lax.rem(x + d, NX)
            settle(pair_r.at[k, to], pair_rs.at[k, d])
            own[k, to] = own[k, to] + pair_r[k, to]

        def e2(k):
            merge_x(k, 2)
            x_send(k, 0)
            x_send(k, 1)
            merge_x(k, 1)
            x_send(k, 2)
            merge_x(k, 3)
            x_send(k, 3)

        def e3(k):
            settle(xb.at[k, 0], x_rs.at[k, 0])
            own[k, right, :, 0:4] = own[k, right, :, 0:4] + xb[k, 0]
            x_send(k, 4)
            settle(xb.at[k, 1], x_rs.at[k, 1])
            own[k, left, :, 4:8] = own[k, left, :, 4:8] + xb[k, 1]
            x_send(k, 5)
            finish.append((xb.at[k], x_ss.at[k]))

        def e4(k):
            merge_x(k, 0)
            settle(xb.at[k, pl.ds(2, 4)], x_rs.at[k, 2])
            own[k, x, :, 0:4] = own[k, x, :, 0:4] + xb[k, 3] + xb[k, 4]
            own[k, x, :, 4:8] = own[k, x, :, 4:8] + xb[k, 2] + xb[k, 5]
            if (c, k) in Y_THEN_Z:
                for d in (4, 3, 5, 2, 6, 1, 7):
                    src = own.at[k, x, :, lax.rem(y + d, NY)]
                    send(src, yz.at[k, d - 1], yz_ss.at[k], yz_rs.at[k], at(dline=2 * d))
                finish.append((yz.at[k], yz_ss.at[k]))
                return
            for d in (2, 1, 3):
                src = own.at[k, x, lax.rem(z + d, NZ)]
                send(src, zr.at[k, d - 1], z_ss.at[k], z_rs.at[k], at(dz=d))
            finish.append((zr.at[k], z_ss.at[k]))

        def to_y(k):
            for d in (4, 3, 5, 2, 6, 1, 7):
                src = own.at[k, x, z, lax.rem(y + d, NY)]
                send(src, yr.at[k, d - 1], y_ss.at[k], y_rs.at[k], at(dline=2 * d))
            finish.append((yr.at[k], y_ss.at[k]))

        def e5(k):
            if (c, k) in Y_THEN_Z:
                settle(yz.at[k], yz_rs.at[k])
                total = own[k, x, :, y]
                for d in range(1, NY):
                    total = total + yz[k, d - 1]
                own[k, x, :, y] = total
                for d in (2, 1, 3):
                    src = own.at[k, x, lax.rem(z + d, NZ), y]
                    send(src, yzz.at[k, d - 1], z_ss.at[k], z_rs.at[k], at(dz=d))
                finish.append((yzz.at[k], z_ss.at[k]))
                return
            settle(zr.at[k], z_rs.at[k])
            own[k, x, z] = own[k, x, z] + zr[k, 0] + zr[k, 1] + zr[k, 2]
            to_y(k)

        def e6(k):
            if (c, k) in Y_THEN_Z:
                settle(yzz.at[k], z_rs.at[k])
                ag[line, k] = own[k, x, z, y] + yzz[k, 0] + yzz[k, 1] + yzz[k, 2]
                return
            settle(yr.at[k], y_rs.at[k])
            total = own[k, x, z, y]
            for d in range(1, NY):
                total = total + yr[k, d - 1]
            ag[line, k] = total

        def a1(k):
            settle(pair_r.at[k], pair_rs.at[k, 0])
            for d in (2, 1, 3, 0):
                to = lax.rem(z + d, NZ)
                own[k, :, to] = own[k, :, to] + pair_r[k, :, to]
                if d:
                    send(own.at[k, :, to], zr1.at[d - 1], zr1_ss.at[0], zr1_rs.at[0], at(dz=d))
            finish.append((zr1, zr1_ss.at[0]))

        def a2(k):
            settle(zr1, zr1_rs.at[0])
            own[k, :, z] = own[k, :, z] + zr1[0] + zr1[1] + zr1[2]
            for d in (2, 1, 3):
                src = own.at[k, lax.rem(x + d, NX), z]
                send(src, xr2.at[d - 1], xr2_ss.at[0], xr2_rs.at[0], at(dx=d))
            finish.append((xr2, xr2_ss.at[0]))

        def a3(k):
            settle(xr2, xr2_rs.at[0])
            own[k, x, z] = own[k, x, z] + xr2[0] + xr2[1] + xr2[2]
            to_y(k)

        slot_of = {3: 0, 2: 1, 6: 2, 1: 3, 7: 4, 5: 5}

        def y_send(k, d):
            src = own.at[k, :, :, lax.rem(y + d, NY)]
            send(src, yr1.at[slot_of[d]], yr1_ss.at[0], yr1_rs.at[0], at(dline=2 * d))

        def b1(k):
            settle(pair_r.at[k], pair_rs.at[k, 0])
            for d in (4, 2, 6, 1, 7, 3, 5, 0):
                to = lax.rem(y + d, NY)
                own[k, :, :, to] = own[k, :, :, to] + pair_r[k, :, :, to]
                if d == 4:
                    send(own.at[k, :, :, to], yrel, yrel_ss.at[0], yrel_rs.at[0], at(dline=NLINE - 2))
                elif d in (2, 6, 1, 7):
                    y_send(k, d)
            finish.append((yrel, yrel_ss.at[0]))

        def relay_y(k):
            settle(yrel, yrel_rs.at[0])
            to = lax.rem(y + 5, NY)
            own[k, :, :, to] = own[k, :, :, to] + yrel[...]
            y_send(k, 5)
            finish.append((yr1, yr1_ss.at[0]))

        def b2(k):
            settle(yr1, yr1_rs.at[0])
            total = own[k, :, :, y]
            for i in range(6):
                total = total + yr1[i]
            own[k, :, :, y] = total
            for d in (2, 1, 3):
                src = own.at[k, lax.rem(x + d, NX), :, y]
                send(src, xr3.at[d - 1], xr3_ss.at[0], xr3_rs.at[0], at(dx=d))
            finish.append((xr3, xr3_ss.at[0]))

        def b3(k):
            settle(xr3, xr3_rs.at[0])
            own[k, x, :, y] = own[k, x, :, y] + xr3[0] + xr3[1] + xr3[2]
            for d in (2, 1, 3):
                src = own.at[k, x, lax.rem(z + d, NZ), y]
                send(src, zr3.at[d - 1], zr3_ss.at[0], zr3_rs.at[0], at(dz=d))
            finish.append((zr3, zr3_ss.at[0]))

        def b4(k):
            settle(zr3, zr3_rs.at[0])
            ag[line, k] = own[k, x, z, y] + zr3[0] + zr3[1] + zr3[2]

        product(order[0])
        pl.semaphore_wait(barrier, 7)
        tell(0)
        send_pair(0)
        for u in range(5):
            src = w_hbm.at[0, :, pl.ds(u * COLS, COLS)]
            pltpu.make_async_copy(src, w_v.at[u], w_sem).start()
        product(order[1])
        product(order[2])
        send_pair(1 if c == 0 else 2)
        e2(0)
        hear(0)
        tell(1)
        product(order[3])
        product(order[4])
        if c == 0:
            b1(2)
            e2(1)
        else:
            send_pair(1)
        hear(1)
        tell(2)
        if c == 0:
            y_send(2, 3)
            e3(0)
            relay_y(2)
            e3(1)
            hear(2)
            e4(0)
            e4(1)
            b2(2)
            e5(0)
            e5(1)
            b3(2)
            e6(0)
            e6(1)
            b4(2)
        else:
            ag[line, 2] = jnp.zeros(TILE, F32)
            a1(1)
            e3(0)
            hear(2)
            e4(0)
            a2(1)
            e5(0)
            a3(1)
            e6(0)
            e6(1)
        for ref, sem in finish:
            settle(ref, sem)

    pl.when(core == 0)(functools.partial(run, 0))
    pl.when(core == 1)(functools.partial(run, 1))

    offsets = [(dm, dx, dz) for dm in range(NM) for dx in range(NX) for dz in range(NZ)][:0:-1]
    shard = ag[line]
    s1[0] = jnp.sum(jnp.sum(shard * shard, axis=0), axis=0, keepdims=True)
    for i, offset in enumerate(offsets):
        send(s1.at[0], s1.at[i + 1], s1_ss.at[0], s1_rs.at[0], at(*offset))
    for d in range(1, NLINE):
        send(ag.at[line], ag.at[line], ag_ss.at[0], ag_rs.at[0], at(dline=d))
    rest1, rest2, rest3 = s1.at[pl.ds(1, len(offsets))], s2.at[pl.ds(1, NLINE - 1)], ag.at[pl.ds(0, NLINE - 1)]
    settle(w_v, w_sem)
    for i in range(3):
        hidden_rows(i)
    settle(rest1, s1_rs.at[0])
    s2[0] = jnp.sum(s1[...], axis=0)
    for d in range(1, NLINE):
        send(s2.at[0], s2.at[d], s2_ss.at[0], s2_rs.at[0], at(dline=d))
    settle(rest1, s1_ss.at[0])
    settle(rest3, ag_rs.at[0])
    settle(rest3, ag_ss.at[0])
    settle(rest2, s2_rs.at[0])
    total = jnp.sum(jnp.sum(s2[...], axis=0), axis=-1, keepdims=True)
    factor = 1.0 / jnp.sqrt(total / entries + 1e-06)
    for c in range(2):
        for k, u in enumerate(UNITS[c]):
            for q in range(NY):
                r, col = (q % 4) * 8, u * COLS + (q // 4) * 128
                out_ref[0, r:r + 8, col:col + 128] = ag[q * 2 + c, k] * factor
    settle(rest2, s2_ss.at[0])
    settle(hid_v, hid_sem)


def store(a_ref, b_ref, a_out, b_out, sem):
    n = b_ref.shape[1] // 2
    copies = [pltpu.make_async_copy(a_ref, a_out, sem.at[2])]
    for i in range(2):
        part = pl.ds(i * n, n)
        copies.append(pltpu.make_async_copy(b_ref.at[0, part], b_out.at[0, part], sem.at[i]))
    for copy in copies:
        copy.start()
    for copy in copies:
        copy.wait()


def on_device(act, dy, w_out, counts):
    rows, hidden = act.shape[1:]
    block = w_out.shape[2]
    entries = NM * hidden * block
    dma = pltpu.SemaphoreType.DMA
    slots = 3
    unit = (NX, NZ, NY) + TILE
    scratch = [
        pltpu.VMEM((rows, hidden), BF16),
        pltpu.VMEM((5, rows, COLS), BF16),
        pltpu.VMEM((5, hidden, COLS), BF16),
        pltpu.VMEM((rows, hidden), BF16),
        pltpu.VMEM((hidden, rows), BF16),
        pltpu.VMEM((slots,) + unit, F32),
        pltpu.VMEM((slots,) + unit, F32),
        pltpu.VMEM((slots,) + unit, F32),
        pltpu.VMEM((2, 6, NZ, 4) + TILE, F32),
        pltpu.VMEM((2, NZ - 1, NY) + TILE, F32),
        pltpu.VMEM((2, NY - 1, NZ) + TILE, F32),
        pltpu.VMEM((2, NZ - 1) + TILE, F32),
        pltpu.VMEM((2, NY - 1) + TILE, F32),
        pltpu.VMEM((NZ - 1, NX, NY) + TILE, F32),
        pltpu.VMEM((NX - 1, NY) + TILE, F32),
        pltpu.VMEM((NX, NZ) + TILE, F32),
        pltpu.VMEM((NY - 2, NX, NZ) + TILE, F32),
        pltpu.VMEM((NX - 1, NZ) + TILE, F32),
        pltpu.VMEM((NZ - 1,) + TILE, F32),
        pltpu.VMEM((NLINE, slots) + TILE, F32),
        pltpu.VMEM((NM * NX * NZ, 1, 128), F32),
        pltpu.VMEM((NLINE, 1, 128), F32),
        dma((6,)), dma((5,)), dma(()), dma(()), pltpu.SemaphoreType.REGULAR((3,)),
        dma((slots,)), dma((slots, 4)),
        dma((2,)), dma((2, 3)),
        dma((2,)), dma((2,)), dma((2,)), dma((2,)), dma((2,)), dma((2,)),
    ] + [dma((1,))] * 18
    shapes = (
        jax.ShapeDtypeStruct((1, hidden // (NX * NZ), block), F32),
        jax.ShapeDtypeStruct((1, rows, hidden), BF16),
    )
    vmem = pl.BlockSpec(memory_space=pltpu.VMEM)
    anywhere = pl.BlockSpec(memory_space=pl.ANY)
    held = [pltpu.with_memory_space_constraint(v, pltpu.HBM) for v in (act, dy, w_out)]
    clipped, back = pl.pallas_call(
        functools.partial(kernel, float(entries)),
        out_shape=shapes,
        in_specs=[pl.BlockSpec(memory_space=pltpu.SMEM)] + [anywhere] * 3,
        out_specs=(vmem, anywhere),
        scratch_shapes=scratch,
        compiler_params=pltpu.CompilerParams(
            collective_id=0, has_side_effects=True, vmem_limit_bytes=48 * 1024 * 1024
        ),
        name="grad_reduce",
    )(counts, *held)
    return pl.pallas_call(
        store,
        out_shape=shapes,
        in_specs=[vmem, vmem],
        out_specs=(anywhere, anywhere),
        scratch_shapes=[dma((3,))],
        name="store",
    )(*[pltpu.with_memory_space_constraint(v, pltpu.VMEM) for v in (clipped, back)])


def solution(mesh):
    in_specs = (
        P("mod", ("loop", "line"), None),
        P("mod", ("loop", "line"), None),
        P("mod", None, None),
        P("mod", "loop", "line"),
    )
    out_specs = (P("mod", "loop", None), P("mod", ("loop", "line"), None))
    return jax.shard_map(
        on_device, mesh=mesh, in_specs=in_specs, out_specs=out_specs, check_vma=False
    )
```
